256 devices in a mesh: section: 8 (over x, core), row: 8 (over z), col: 4 (over y).
Axes of the slice: x: 4, y: 4, z: 8, core: 2. Of those that a mesh axis runs over, the one named last changes fastest.
Arguments:
- frames: bfloat16 [2, 6, 16, 64, 128], P(None, None, None, 'row', 'col'), may hold values from -6 to 6
- region_order: int32 [6], replicated, may hold values from 0 to 5, each once
- encoder: bfloat16 [64, 16], replicated, may hold values from -1.5 to 1.5
- input_kernel: bfloat16 [8, 448, 1600], P('section'), may hold values from -0.15625 to 0.15625
- hidden_kernel: bfloat16 [8, 256, 1600], P('section'), may hold values from -0.15625 to 0.15625
- memory_kernel: bfloat16 [8, 192, 1600], P('section'), may hold values from -0.15625 to 0.15625
- output_kernel: bfloat16 [8, 64, 3200], P('section'), may hold values from -0.109375 to 0.109375
- mixing_weight: bfloat16 [8, 64, 128], P('section'), may hold values from -0.5 to 0.5
- hidden_start: float32 [8, 3, 64, 64, 128], P('section', None, None, 'row', 'col'), may hold values from -0.9 to 0.9
- cell_start: float32 [8, 3, 64, 64, 128], P('section', None, None, 'row', 'col'), may hold values from -5 to 5
- memory_start: float32 [3, 64, 64, 128], P(None, None, 'row', 'col'), may hold values from -5 to 5
Outputs:
- hidden_final: float32 [8, 3, 64, 64, 128], P('section', None, None, 'row', 'col')
- cell_final: float32 [8, 3, 64, 64, 128], P('section', None, None, 'row', 'col')
- memory_final: float32 [8, 3, 64, 64, 128], P('section', None, None, 'row', 'col')
The draws below stay inside these ranges and needn't reach their ends.
Inputs may be any that keep to these rules, and one draw needn't show every extreme that they name: A permutation of the regions; micro-batch b takes region region_order[b] for b < 3, the rest are unused.
All inputs are finite; a program needn't handle non-finite values.
Results may differ from the reference program's by a relative error of at most 0.017.
Values may be sent and summed in bfloat16 or wider, within the bound.
A program may use at most 64 MiB of HBM per device.

```python
import jax
import jax.numpy as jnp
from jax import lax

HID = 64
PATCH_CH = 16
KS = 5
MB = 3
STEPS = 2
LAYERS = 8
REGIONS = 6
HEIGHT = 64
WIDTH = 128


def block_levels(stream_key, dims, split, low, top_value):
    factor_of = 1.0
    for position, parts in split:
        steps = jax.random.uniform(jax.random.fold_in(jax.random.fold_in(stream_key, 6), position), (parts,), jnp.float32, low / len(split), top_value / len(split))
        factor_of = factor_of * jnp.repeat(jnp.exp(steps), dims[position] // parts).reshape((-1,) + (1,) * (len(dims) - 1 - position))
    return factor_of


def normal_values(stream_key, dims, scale, bound, pieces=(), kind=jnp.bfloat16):
    factor_of = block_levels(stream_key, dims, pieces, -0.22, 0.18) if pieces else 1.0
    drawn = jax.random.normal(stream_key, dims, jnp.float32) * scale * factor_of
    return jnp.minimum(jnp.maximum(drawn, -bound), bound).astype(kind)


def setup_inputs(seed: int = 0) -> dict:
    streams_of = jax.random.split(jax.random.key(seed), 12)
    frames = normal_values(streams_of[0], (STEPS, REGIONS, PATCH_CH, HEIGHT, WIDTH), 1.0, 6.0, ((3, 8), (4, 4)))
    region_order = jax.random.permutation(streams_of[1], REGIONS).astype(jnp.int32)
    encoder = normal_values(streams_of[2], (HID, PATCH_CH), PATCH_CH ** -0.5, 1.5)
    input_kernel = normal_values(streams_of[3], (LAYERS, 7 * HID, KS * KS * HID), (KS * KS * HID) ** -0.5, 0.15625, ((0, 8),))
    hidden_kernel = normal_values(streams_of[4], (LAYERS, 4 * HID, KS * KS * HID), (KS * KS * HID) ** -0.5, 0.15625, ((0, 8),))
    memory_kernel = normal_values(streams_of[5], (LAYERS, 3 * HID, KS * KS * HID), (KS * KS * HID) ** -0.5, 0.15625, ((0, 8),))
    output_kernel = normal_values(streams_of[6], (LAYERS, HID, KS * KS * 2 * HID), (KS * KS * 2 * HID) ** -0.5, 0.109375, ((0, 8),))
    mixing_weight = normal_values(streams_of[7], (LAYERS, HID, 2 * HID), (2 * HID) ** -0.5, 0.5, ((0, 8),))
    hidden_start = jnp.clip(jax.random.uniform(streams_of[8], (LAYERS, MB, HID, HEIGHT, WIDTH), jnp.float32, -0.9, 0.9) * block_levels(streams_of[8], (LAYERS, MB, HID, HEIGHT, WIDTH), ((0, 8), (3, 8), (4, 4)), -0.4, 0.0), -0.9, 0.9)
    cell_start = normal_values(streams_of[9], (LAYERS, MB, HID, HEIGHT, WIDTH), 1.0, 5.0, ((0, 8), (3, 8), (4, 4)), jnp.float32)
    memory_start = normal_values(streams_of[10], (MB, HID, HEIGHT, WIDTH), 1.0, 5.0, ((2, 8), (3, 4)), jnp.float32)
    return {"frames": frames, "region_order": region_order, "encoder": encoder, "input_kernel": input_kernel, "hidden_kernel": hidden_kernel, "memory_kernel": memory_kernel, "output_kernel": output_kernel, "mixing_weight": mixing_weight, "hidden_start": hidden_start, "cell_start": cell_start, "memory_start": memory_start}


def convolve(field, kernel):
    out_channels = kernel.shape[0]
    in_channels = field.shape[0]
    filters = kernel.astype(jnp.float32).reshape(out_channels, KS, KS, in_channels).transpose(0, 3, 1, 2)
    margin = KS // 2
    result = lax.conv_general_dilated(field.astype(jnp.float32)[None], filters, (1, 1), ((margin, margin), (margin, margin)), dimension_numbers=("NCHW", "OIHW", "NCHW"), precision=lax.Precision.HIGHEST)
    return result[0]


def memory_cell(layer_input, hidden_prev, cell_prev, memory_in, input_kernel, hidden_kernel, memory_kernel, output_kernel, mixing_weight):
    sigmoid = jax.nn.sigmoid
    from_input = convolve(layer_input, input_kernel).reshape(7, HID, HEIGHT, WIDTH)
    from_hidden = convolve(hidden_prev.astype(jnp.bfloat16), hidden_kernel).reshape(4, HID, HEIGHT, WIDTH)
    from_memory = convolve(memory_in.astype(jnp.bfloat16), memory_kernel).reshape(3, HID, HEIGHT, WIDTH)
    cell_new = sigmoid(from_input[1] + from_hidden[1] + 1.0) * cell_prev + sigmoid(from_input[0] + from_hidden[0]) * jnp.tanh(from_input[2] + from_hidden[2])
    memory_new = sigmoid(from_input[4] + from_memory[1] + 1.0) * memory_in + sigmoid(from_input[3] + from_memory[0]) * jnp.tanh(from_input[5] + from_memory[2])
    joined = jnp.concatenate([cell_new, memory_new], 0).astype(jnp.bfloat16)
    out_gate = sigmoid(from_input[6] + from_hidden[3] + convolve(joined, output_kernel))
    mixed = jnp.dot(mixing_weight, joined.reshape(2 * HID, HEIGHT * WIDTH), preferred_element_type=jnp.float32).reshape(HID, HEIGHT, WIDTH)
    return out_gate * jnp.tanh(mixed), cell_new, memory_new


def reference(frames, region_order, encoder, input_kernel, hidden_kernel, memory_kernel, output_kernel, mixing_weight, hidden_start, cell_start, memory_start):
    hidden_states = [[hidden_start[layer_index, batch_index] for batch_index in range(MB)] for layer_index in range(LAYERS)]
    cell_states = [[cell_start[layer_index, batch_index] for batch_index in range(MB)] for layer_index in range(LAYERS)]
    memory_last = [[memory_start[batch_index] for batch_index in range(MB)] for layer_index in range(LAYERS)]
    carried = [memory_start[batch_index] for batch_index in range(MB)]
    for moment in range(STEPS):
        for batch_index in range(MB):
            frame_now = frames[moment, region_order[batch_index]]
            layer_input = jnp.dot(encoder, frame_now.reshape(PATCH_CH, HEIGHT * WIDTH), preferred_element_type=jnp.float32).astype(jnp.bfloat16).reshape(HID, HEIGHT, WIDTH)
            memory_in = carried[batch_index]
            for layer_index in range(LAYERS):
                hidden_new, cell_new, memory_new = memory_cell(layer_input, hidden_states[layer_index][batch_index], cell_states[layer_index][batch_index], memory_in, input_kernel[layer_index], hidden_kernel[layer_index], memory_kernel[layer_index], output_kernel[layer_index], mixing_weight[layer_index])
                hidden_states[layer_index][batch_index] = hidden_new
                cell_states[layer_index][batch_index] = cell_new
                memory_last[layer_index][batch_index] = memory_new
                layer_input = hidden_new.astype(jnp.bfloat16)
                memory_in = memory_new
            carried[batch_index] = memory_in
    hidden_final = jnp.stack([jnp.stack(row_list) for row_list in hidden_states])
    cell_final = jnp.stack([jnp.stack(row_list) for row_list in cell_states])
    memory_final = jnp.stack([jnp.stack(row_list) for row_list in memory_last])
    return (hidden_final, cell_final, memory_final)
```

```python
import functools

import jax
import jax.numpy as jnp
from jax import lax
from jax.experimental import pallas as pl
from jax.experimental.pallas import tpu as pltpu
from jax.sharding import PartitionSpec as P

KS = 5
HALO = 4
SIDE = 16
EDGE = 8
DIRS = [(dr, dc) for dr in (-1, 0, 1) for dc in (-1, 0, 1)]
MESH = pl.DeviceIdType.MESH


def sigmoid(value):
    return 0.5 * jnp.tanh(0.5 * value) + 0.5


def kernel_body(
    sections,
    rows,
    cols,
    steps,
    batches,
    enc_ref,
    hid_ref,
    cel_ref,
    mem_ref,
    wx_ref,
    wh_ref,
    wm_ref,
    wo_ref,
    wmix_ref,
    outh_ref,
    outs_ref,
    xwin,
    mwin,
    hwin,
    cwin,
    wide,
    p01,
    p23,
    p4,
    acc,
    state,
    joined,
    js,
    hbuf,
    mbuf,
    e_send,
    f_send,
    i_send,
    x_send,
    x_recv,
    m_send,
    m_recv,
    h_send,
    h_recv,
    c_send,
    c_recv,
    o_sem,
):
    sec = lax.axis_index("section")
    row = lax.axis_index("row")
    col = lax.axis_index("col")
    tr, tc = enc_ref.shape[1], enc_ref.shape[2]
    gr, gc = tr + 4, tc + 2 * EDGE
    wr = tr + 2 * HALO
    items = steps * batches
    first = sec == 0
    last = sec == sections - 1
    after = lax.rem(sec + 1, sections)
    before = lax.rem(sec + sections - 1, sections)

    def exists(dr, dc):
        found = None
        for ok in (
            row > 0 if dr < 0 else row < rows - 1 if dr > 0 else None,
            col > 0 if dc < 0 else col < cols - 1 if dc > 0 else None,
        ):
            if ok is not None:
                found = ok if found is None else found & ok
        return found

    def guarded(cond, fn):
        if cond is None:
            fn()
        else:
            pl.when(cond)(fn)

    def both(a, b):
        return b if a is None else a if b is None else a & b

    def src_part(dr, dc):
        rs = pl.ds(0, HALO) if dr < 0 else pl.ds(tr - HALO, HALO) if dr > 0 else pl.ds(0, tr)
        cs = pl.ds(0, SIDE) if dc < 0 else pl.ds(tc - SIDE, SIDE) if dc > 0 else pl.ds(0, tc)
        return rs, cs

    def dst_part(dr, dc):
        rs = pl.ds(HALO + tr, HALO) if dr < 0 else pl.ds(0, HALO) if dr > 0 else pl.ds(HALO, tr)
        cs = pl.ds(SIDE + tc, SIDE) if dc < 0 else pl.ds(0, SIDE) if dc > 0 else pl.ds(SIDE, tc)
        return rs, cs

    def copy_of(src, src_item, dst, dst_item, send_sem, recv_sem, target, index):
        dr, dc = DIRS[index]
        srs, scs = src_part(dr, dc)
        drs, dcs = dst_part(dr, dc)
        return pltpu.make_async_remote_copy(
            src_ref=src.at[src_item, srs, scs],
            dst_ref=dst.at[dst_item, drs, dcs],
            send_sem=send_sem.at[src_item, index],
            recv_sem=recv_sem.at[dst_item, index],
            device_id={
                "section": target,
                "row": lax.rem(row + dr + rows, rows),
                "col": lax.rem(col + dc + cols, cols),
            },
            device_id_type=MESH,
        )

    def each(indices, cond, fn):
        for index in indices:
            guarded(both(cond, exists(*DIRS[index])), functools.partial(fn, index))

    def each_source(indices, cond, fn):
        for index in indices:
            dr, dc = DIRS[index]
            guarded(both(cond, exists(-dr, -dc)), functools.partial(fn, index))

    every = list(range(9))
    around = [i for i in every if DIRS[i] != (0, 0)]
    centre = [DIRS.index((0, 0))]

    centre_rows, centre_cols = pl.ds(HALO, tr), pl.ds(SIDE, tc)

    def clear(k, _):
        zero = jnp.zeros(xwin.shape[1:], jnp.bfloat16)
        xwin[k] = zero
        mwin[k] = zero
        hwin[k] = zero
        return 0

    lax.fori_loop(0, items, clear, 0)

    def clear_cells(b, _):
        cwin[b] = jnp.zeros(cwin.shape[1:], jnp.float32)
        return 0

    lax.fori_loop(0, batches, clear_cells, 0)
    js[:, gr] = jnp.zeros((KS, tc, 128), jnp.bfloat16)

    barrier = pltpu.get_barrier_semaphore()
    for index in every:
        dr, dc = DIRS[index]

        def greet(dr=dr, dc=dc):
            for target in (after, before) + (() if (dr, dc) == (0, 0) else (sec,)):
                pl.semaphore_signal(
                    barrier,
                    inc=1,
                    device_id={"section": target, "row": row + dr, "col": col + dc},
                    device_id_type=MESH,
                )

        guarded(exists(dr, dc), greet)
    near_rows = 1 + (row > 0).astype(jnp.int32) + (row < rows - 1).astype(jnp.int32)
    near_cols = 1 + (col > 0).astype(jnp.int32) + (col < cols - 1).astype(jnp.int32)
    pl.semaphore_wait(barrier, 3 * near_rows * near_cols - 1)

    def x_first(k, index):
        return copy_of(enc_ref, k, xwin, k, e_send, x_recv, sec, index)

    def m_first(b, index):
        return copy_of(mem_ref, b, mwin, b, f_send, m_recv, sec, index)

    def h_first(b, index):
        return copy_of(hid_ref, b, hwin, b, i_send, h_recv, sec, index)

    def c_first(b, index):
        return copy_of(cel_ref, b, cwin, b, c_send, c_recv, sec, index)

    def x_next(k, index):
        return copy_of(hbuf, k, xwin, k, x_send, x_recv, after, index)

    def m_next(k, index):
        return copy_of(mbuf, k, mwin, k, m_send, m_recv, after, index)

    def m_loop(k, index):
        return copy_of(mbuf, k, mwin, k + batches, m_send, m_recv, after, index)

    def h_next(k, index):
        return copy_of(hbuf, k, hwin, k + batches, h_send, h_recv, sec, index)

    def h_own(k):
        return pltpu.make_async_copy(
            hbuf.at[k], hwin.at[k + batches, centre_rows, centre_cols], o_sem.at[k]
        )

    def start(make, k):
        return lambda index: make(k, index).start()

    def sent(make, k):
        return lambda index: make(k, index).wait_send()

    def landed(make, k):
        return lambda index: make(k, index).wait_recv()

    def begin(b, _):
        each(around, first, start(x_first, b))
        each(around, first, start(m_first, b))
        each(around, None, start(h_first, b))
        each(around, None, start(c_first, b))
        return 0

    lax.fori_loop(0, batches, begin, 0)

    def begin_later(k, _):
        each(around, first, start(x_first, k))
        return 0

    lax.fori_loop(batches, items, begin_later, 0)

    def place(b, _):
        hwin[b, centre_rows, centre_cols] = hid_ref[b]
        cwin[b, centre_rows, centre_cols] = cel_ref[b]
        return 0

    lax.fori_loop(0, batches, place, 0)

    @pl.when(first)
    def _():
        def place_first(b, _):
            mwin[b, centre_rows, centre_cols] = mem_ref[b]
            return 0

        lax.fori_loop(0, batches, place_first, 0)

        def place_input(k, _):
            xwin[k, centre_rows, centre_cols] = enc_ref[k]
            return 0

        lax.fori_loop(0, items, place_input, 0)

    low_lane = lax.broadcasted_iota(jnp.int32, (1, 1, 128), 2) < 64
    start_col = SIDE - EDGE - 2

    def spread(window):
        for r in range(wr):
            wide[r] = window[r].astype(jnp.float32)
        for r in range(wr):
            taps = [wide[r, pl.ds(start_col + q, gc), :] for q in range(KS)]
            p01[r] = jnp.where(low_lane[0], taps[0], taps[1]).astype(jnp.bfloat16)
            p23[r] = jnp.where(low_lane[0], taps[2], taps[3]).astype(jnp.bfloat16)
            below = wide[min(r + 1, wr - 1), pl.ds(start_col + 4, gc), :]
            p4[r] = jnp.where(low_lane[0], taps[4], below).astype(jnp.bfloat16)

    def patches():
        parts = []
        for p in range(KS):
            parts.append(p01[p : p + gr].reshape(gr * gc, 128))
            parts.append(p23[p : p + gr].reshape(gr * gc, 128))
        for p in (0, 2, 4):
            parts.append(p4[p : p + gr].reshape(gr * gc, 128))
        return jnp.concatenate(parts, axis=1)

    def cell(k, _):
        b = lax.rem(k, batches)
        early = k < batches
        late = k >= batches

        each_source(around, early, landed(h_first, b))
        each_source(around, late, landed(h_next, b))
        pl.when(late)(lambda: h_own(b).wait())
        spread(hwin.at[k])
        acc[...] = jnp.dot(patches(), wh_ref[...], preferred_element_type=jnp.float32)

        @pl.when(early)
        def _():
            each_source(around, None, landed(c_first, b))
            for r in range(gr):
                state[b, r] = cwin[b, r + HALO - 2, pl.ds(SIDE - EDGE, gc), :]

        each_source(around, first & early, landed(m_first, b))
        each_source(every, jnp.logical_not(first) | late, landed(m_next, k))
        spread(mwin.at[k])
        acc[...] += jnp.dot(patches(), wm_ref[...], preferred_element_type=jnp.float32)
        for r in range(gr):
            memory = wide[r + HALO - 2, pl.ds(SIDE - EDGE, gc), :]
            state[b, r] = jnp.where(low_lane[0], state[b, r], memory)

        each_source(around, first, landed(x_first, k))
        each_source(every, jnp.logical_not(first), landed(x_next, k))
        spread(xwin.at[k])
        acc[...] += jnp.dot(patches(), wx_ref[...], preferred_element_type=jnp.float32)

        grid_col = lax.broadcasted_iota(jnp.int32, (gc, 1), 0) + (col * tc - EDGE)
        col_ok = (grid_col >= 0) & (grid_col < cols * tc)
        for r in range(gr):
            part = acc[r * gc : (r + 1) * gc, :]
            new = sigmoid(part[:, 128:256] + 1.0) * state[b, r] + sigmoid(part[:, :128]) * jnp.tanh(
                part[:, 256:384]
            )
            state[b, r] = new
            grid_row = row * tr + (r - 2)
            ok = col_ok & ((grid_row >= 0) & (grid_row < rows * tr))
            joined[r] = jnp.where(ok, new, 0.0)

        tile = state[b, 2 : 2 + tr, EDGE : EDGE + tc, :]
        turned = pltpu.roll(tile.reshape(tr * tc, 128), 64, 1).reshape(tr, tc, 128)
        mbuf[k] = jnp.where(low_lane, turned, tile).astype(jnp.bfloat16)
        each(every, jnp.logical_not(last), start(m_next, k))
        each(every, last & early, start(m_loop, k))

        for q in range(KS):
            for r in range(gr):
                js[q, r] = joined[r, pl.ds(EDGE - 2 + q, tc), :].astype(jnp.bfloat16)
        parts = [
            js[q, 2 * g : 2 * g + tr + 1].reshape((tr + 1) * tc, 128)
            for g in range(3)
            for q in range(KS)
        ]
        out = jnp.dot(
            jnp.concatenate(parts, axis=1), wo_ref[...], preferred_element_type=jnp.float32
        )
        mixed = jnp.dot(
            js[2, 2 : 2 + tr].reshape(tr * tc, 128),
            wmix_ref[...],
            preferred_element_type=jnp.float32,
        )
        gate = out[: tr * tc, :128] + out[tc:, 128:]
        gate = gate.reshape(tr, tc, 128) + acc[2 * gc : (2 + tr) * gc, 384:].reshape(tr, gc, 128)[
            :, EDGE : EDGE + tc
        ]
        hidden = sigmoid(gate) * jnp.tanh(mixed).reshape(tr, tc, 128)
        hbuf[k] = hidden.astype(jnp.bfloat16)
        each(every, jnp.logical_not(last), start(x_next, k))

        @pl.when(early)
        def _():
            each(around, None, start(h_next, k))
            h_own(k).start()

        @pl.when(late)
        def _():
            outh_ref[b] = hidden
            outs_ref[b] = state[b, 2 : 2 + tr, EDGE : EDGE + tc, :]

        return 0

    lax.fori_loop(0, items, cell, 0)

    def finish(k, _):
        each(around, first, sent(x_first, k))
        each(every, jnp.logical_not(last), sent(x_next, k))
        each(every, jnp.logical_not(last), sent(m_next, k))
        return 0

    def finish_early(b, _):
        each(around, first, sent(m_first, b))
        each(every, last, sent(m_loop, b))
        each(around, None, sent(h_first, b))
        each(around, None, sent(h_next, b))
        each(around, None, sent(c_first, b))
        return 0

    lax.fori_loop(0, items, finish, 0)
    lax.fori_loop(0, batches, finish_early, 0)


def taps_first(blocks):
    turned = jnp.concatenate(blocks, 0).transpose(1, 2, 3, 0)
    wide = turned.shape[3]
    return jnp.concatenate(
        [
            turned[:, :4].reshape(-1, wide),
            turned[:, 4].reshape(-1, wide),
            jnp.zeros((turned.shape[2], wide), turned.dtype),
        ],
        0,
    )


def per_device(
    sizes,
    frames,
    region_order,
    encoder,
    input_kernel,
    hidden_kernel,
    memory_kernel,
    output_kernel,
    mixing_weight,
    hidden_start,
    cell_start,
    memory_start,
):
    bf16, f32 = jnp.bfloat16, jnp.float32
    sections, rows, cols = sizes
    steps, _, patch, tr, tc = frames.shape
    batches, ch = memory_start.shape[:2]
    items = steps * batches
    gr, gc = tr + 4, tc + 2 * EDGE
    wr, wc = tr + 2 * HALO, tc + 2 * SIDE

    ik = input_kernel[0].reshape(7, ch, KS, KS, ch)
    hk = hidden_kernel[0].reshape(4, ch, KS, KS, ch)
    mk = memory_kernel[0].reshape(3, ch, KS, KS, ch)
    none = jnp.zeros_like(ik[0])
    wx = taps_first([ik[0], ik[3], ik[1], ik[4], ik[2], ik[5], ik[6], ik[6]])
    wh = taps_first([hk[0], none, hk[1], none, hk[2], none, hk[3], hk[3]])
    wm = taps_first([none, mk[0], none, mk[1], none, mk[2], none, none])
    ok = output_kernel[0].reshape(ch, KS, KS, 2 * ch).transpose(1, 2, 3, 0)
    ok = jnp.concatenate([ok, jnp.zeros_like(ok[:1])], 0).reshape(3, 2, KS, 2 * ch, ch)
    wo = jnp.concatenate([ok[:, 0], ok[:, 0], ok[:, 1], ok[:, 1]], -1).reshape(-1, 4 * ch)
    wmix = jnp.concatenate([mixing_weight[0], mixing_weight[0]], 0).T

    def twice(value):
        return jnp.concatenate([value, value], -1)

    picked = jnp.take(frames, region_order[:batches], axis=1)
    enc = jnp.einsum("tbcyx,oc->tbyxo", picked, encoder, preferred_element_type=f32)
    enc = twice(enc.astype(bf16)).reshape(items, tr, tc, 2 * ch)
    hid = twice(hidden_start[0].transpose(0, 2, 3, 1).astype(bf16))
    cel = twice(cell_start[0].transpose(0, 2, 3, 1))
    mem = twice(memory_start.transpose(0, 2, 3, 1).astype(bf16))

    vmem = pl.BlockSpec(memory_space=pltpu.VMEM)
    dma = pltpu.SemaphoreType.DMA
    ends = jax.ShapeDtypeStruct((batches, tr, tc, 2 * ch), f32)
    outh, outs = pl.pallas_call(
        functools.partial(kernel_body, sections, rows, cols, steps, batches),
        out_shape=(ends, ends),
        in_specs=[vmem] * 9,
        out_specs=(vmem, vmem),
        scratch_shapes=[
            pltpu.VMEM((items, wr, wc, 128), bf16),
            pltpu.VMEM((items, wr, wc, 128), bf16),
            pltpu.VMEM((items, wr, wc, 128), bf16),
            pltpu.VMEM((batches, wr, wc, 128), f32),
            pltpu.VMEM((wr, wc, 128), f32),
            pltpu.VMEM((wr, gc, 128), bf16),
            pltpu.VMEM((wr, gc, 128), bf16),
            pltpu.VMEM((wr, gc, 128), bf16),
            pltpu.VMEM((gr * gc, 512), f32),
            pltpu.VMEM((batches, gr, gc, 128), f32),
            pltpu.VMEM((gr, gc, 128), f32),
            pltpu.VMEM((KS, gr + 1, tc, 128), bf16),
            pltpu.VMEM((items, tr, tc, 128), bf16),
            pltpu.VMEM((items, tr, tc, 128), bf16),
            dma((items, 9)),
            dma((batches, 9)),
            dma((batches, 9)),
            dma((items, 9)),
            dma((items, 9)),
            dma((items, 9)),
            dma((items, 9)),
            dma((batches, 9)),
            dma((items, 9)),
            dma((batches, 9)),
            dma((batches, 9)),
            dma((batches,)),
        ],
        compiler_params=pltpu.CompilerParams(
            collective_id=0, has_side_effects=True, vmem_limit_bytes=56 << 20
        ),
        name="predrnn",
    )(enc, hid, cel, mem, wx, wh, wm, wo, wmix)

    def back(value):
        return value.transpose(0, 3, 1, 2)[None]

    return back(outh[..., :ch]), back(outs[..., :ch]), back(outs[..., ch:])


def solution(mesh):
    sizes = tuple(mesh.shape[name] for name in ("section", "row", "col"))
    return jax.shard_map(
        functools.partial(per_device, sizes),
        mesh=mesh,
        in_specs=(
            P(None, None, None, "row", "col"),
            P(),
            P(),
            P("section", None, None),
            P("section", None, None),
            P("section", None, None),
            P("section", None, None),
            P("section", None, None),
            P("section", None, None, "row", "col"),
            P("section", None, None, "row", "col"),
            P(None, None, "row", "col"),
        ),
        out_specs=(
            P("section", None, None, "row", "col"),
            P("section", None, None, "row", "col"),
            P("section", None, None, "row", "col"),
        ),
        check_vma=False,
    )
```

```python
import functools

import jax
import jax.numpy as jnp
from jax import lax
from jax.experimental import pallas as pl
from jax.experimental.pallas import tpu as pltpu
from jax.sharding import PartitionSpec as P

KS = 5
HALO = 4
SIDE = 16
EDGE = 8
CH = 64
DIRS = [(-1, -1), (-1, 1), (1, -1), (1, 1), (0, -1), (0, 1), (-1, 0), (1, 0), (0, 0)]
AROUND = list(range(8))
EVERY = list(range(9))
MESH = pl.DeviceIdType.MESH

SLABS = {
    (0, 0): (0, 4, 8),
    (1, 0): (4, 0, 4),
    (-1, 0): (0, 12, 4),
    (0, 1): (13, 17, 2),
    (1, 1): (15, 16, 1),
    (-1, 1): (12, 19, 1),
    (0, -1): (9, 21, 2),
    (1, -1): (11, 20, 1),
    (-1, -1): (8, 23, 1),
}
STRIP_ROWS = [((0, 1), (2, 3)), ((0, 1), (4, 5)), ((2, 3), (6, 7)), ((4, 5), (6, 7))]
WINDOW_ROWS = [((0, 1), (2, 3)), ((4, 5), (8, 9)), ((6, 7), (10, 11)), ((12, 13), (14, 15))]


def sigmoid(value):
    return 0.5 * jnp.tanh(0.5 * value) + 0.5


def dot_last(left, right):
    return lax.dot_general(
        left, right, (((1,), (1,)), ((), ())), preferred_element_type=jnp.float32
    )


def kernel_body(
    sections,
    rows,
    cols,
    steps,
    batches,
    enc_ref,
    hid_ref,
    cel_ref,
    mem_ref,
    ik_ref,
    hk_ref,
    mk_ref,
    ok_ref,
    mix_ref,
    outh_ref,
    outs_ref,
    xwin,
    mwin,
    hwin,
    cwin,
    epack,
    hpack,
    cpack,
    mpack,
    hbuf,
    mbuf,
    wide,
    p01,
    p23,
    p40,
    p12,
    p34,
    acc_x,
    acc_h,
    acc_m,
    state,
    joined,
    js,
    wx,
    wh,
    wm,
    wo,
    wmix,
    w_sem,
    e_send,
    f_send,
    i_send,
    x_send,
    x_recv,
    m_send,
    m_recv,
    h_send,
    h_recv,
    c_send,
    c_recv,
    o_sem,
):
    bf16, f32 = jnp.bfloat16, jnp.float32
    sec = lax.axis_index("section")
    row = lax.axis_index("row")
    col = lax.axis_index("col")
    tr, tc = enc_ref.shape[1], enc_ref.shape[2]
    gr, gc = tr + 4, tc + 2 * EDGE
    wr = tr + 2 * HALO
    items = steps * batches
    first = sec == 0
    last = sec == sections - 1
    after = lax.rem(sec + 1, sections)
    before = lax.rem(sec + sections - 1, sections)

    def block(n, size=CH):
        return pl.ds(n * size, size)

    fetches = []

    def fetch(source, target):
        fetches.append(pltpu.make_async_copy(source, target, w_sem.at[len(fetches)]))

    fetch(hk_ref, wh)
    for place, gate in ((0, 1), (1, 0), (3, 2)):
        fetch(mk_ref.at[block(gate)], wm.at[block(place)])
    for place, gate in enumerate((0, 3, 1, 4, 2, 5, 6, 6)):
        fetch(ik_ref.at[block(gate)], wx.at[block(place)])
    half = KS * 2 * CH
    for p in range(KS):
        for copy in (0, 1):
            fetch(
                ok_ref.at[:, block(p, half)],
                wo.at[block(2 * (p % 2) + copy), block(p // 2, half)],
            )
    for copy in (0, 1):
        fetch(mix_ref, wmix.at[block(copy)])
    for copy in fetches:
        copy.start()

    def exists(dr, dc):
        found = None
        for ok in (
            row > 0 if dr < 0 else row < rows - 1 if dr > 0 else None,
            col > 0 if dc < 0 else col < cols - 1 if dc > 0 else None,
        ):
            if ok is not None:
                found = ok if found is None else found & ok
        return found

    def guarded(cond, fn):
        if cond is None:
            fn()
        else:
            pl.when(cond)(fn)

    def both(a, b):
        return b if a is None else a if b is None else a & b

    def copy_of(src, src_item, dst, dst_item, send_sem, recv_sem, target, index):
        dr, dc = DIRS[index]
        from_slab, to_slab, count = SLABS[(dr, dc)]
        return pltpu.make_async_remote_copy(
            src_ref=src.at[src_item, pl.ds(from_slab, count)],
            dst_ref=dst.at[dst_item, pl.ds(to_slab, count)],
            send_sem=send_sem.at[src_item, index],
            recv_sem=recv_sem.at[dst_item, index],
            device_id={
                "section": target,
                "row": lax.rem(row + dr + rows, rows),
                "col": lax.rem(col + dc + cols, cols),
            },
            device_id_type=MESH,
        )

    def each(indices, cond, fn):
        for index in indices:
            guarded(both(cond, exists(*DIRS[index])), functools.partial(fn, index))

    def each_source(indices, cond, fn):
        for index in indices:
            dr, dc = DIRS[index]
            guarded(both(cond, exists(-dr, -dc)), functools.partial(fn, index))

    def clear(k, _):
        zero = jnp.zeros(xwin.shape[1:], bf16)
        xwin[k] = zero
        mwin[k] = zero
        hwin[k] = zero
        return 0

    lax.fori_loop(0, items, clear, 0)

    def clear_cells(b, _):
        cwin[b] = jnp.zeros(cwin.shape[1:], bf16)
        return 0

    lax.fori_loop(0, batches, clear_cells, 0)

    barrier = pltpu.get_barrier_semaphore()
    for index in EVERY:
        dr, dc = DIRS[index]

        def greet(dr=dr, dc=dc):
            for target in (after, before) + (() if (dr, dc) == (0, 0) else (sec,)):
                pl.semaphore_signal(
                    barrier,
                    inc=1,
                    device_id={"section": target, "row": row + dr, "col": col + dc},
                    device_id_type=MESH,
                )

        guarded(exists(dr, dc), greet)

    js[:, gr] = jnp.zeros((KS, tc, 128), bf16)
    wide[...] = jnp.zeros(wide.shape, f32)
    wm[block(2), :] = jnp.zeros((CH, wm.shape[1]), bf16)
    wo[block(1, 2 * CH), block(2, half)] = jnp.zeros((2 * CH, half), bf16)

    low = lax.broadcasted_iota(jnp.int32, (1, 128), 1) < CH

    def pack(value_of, store):
        line = [value_of(r) for r in range(tr)]
        for r in range(tr):
            store(r, jnp.where(low, line[r][:16], line[r][16:32]).astype(bf16))
        for side, begin in ((8, 0), (12, tc - EDGE)):
            strip = [part[begin : begin + EDGE] for part in line]
            for slab, (lo, hi) in enumerate(STRIP_ROWS):
                upper = jnp.concatenate([strip[lo[0]], strip[lo[1]]], 0)
                lower = jnp.concatenate([strip[hi[0]], strip[hi[1]]], 0)
                store(side + slab, jnp.where(low, upper, lower).astype(bf16))

    def pack_into(target, item, value_of):
        def store(slab, value):
            target[item, slab] = value

        pack(value_of, store)

    def pack_first(b, _):
        pack_into(hpack, b, lambda r: hid_ref[b, r].astype(f32))
        pack_into(mpack, b, lambda r: mem_ref[b, r].astype(f32))
        pack_into(cpack, b, lambda r: cel_ref[b, r])
        return 0

    lax.fori_loop(0, batches, pack_first, 0)

    def pack_inputs(k, _):
        pack_into(epack, k, lambda r: enc_ref[k, r].astype(f32))
        return 0

    lax.fori_loop(0, items, pack_inputs, 0)

    near_rows = 1 + (row > 0).astype(jnp.int32) + (row < rows - 1).astype(jnp.int32)
    near_cols = 1 + (col > 0).astype(jnp.int32) + (col < cols - 1).astype(jnp.int32)
    pl.semaphore_wait(barrier, 3 * near_rows * near_cols - 1)

    def x_first(k, index):
        return copy_of(epack, k, xwin, k, e_send, x_recv, sec, index)

    def m_first(b, index):
        return copy_of(mpack, b, mwin, b, f_send, m_recv, sec, index)

    def h_first(b, index):
        return copy_of(hpack, b, hwin, b, i_send, h_recv, sec, index)

    def c_first(b, index):
        return copy_of(cpack, b, cwin, b, c_send, c_recv, sec, index)

    def x_next(k, index):
        return copy_of(hbuf, k, xwin, k, x_send, x_recv, after, index)

    def m_next(k, index):
        return copy_of(mbuf, k, mwin, k, m_send, m_recv, after, index)

    def m_loop(k, index):
        return copy_of(mbuf, k, mwin, k + batches, m_send, m_recv, after, index)

    def h_next(k, index):
        return copy_of(hbuf, k, hwin, k + batches, h_send, h_recv, sec, index)

    def own(src, src_item, dst, dst_item, sem):
        return pltpu.make_async_copy(
            src.at[src_item, pl.ds(0, tr)], dst.at[dst_item, pl.ds(HALO, tr)], sem
        )

    def x_own(k):
        return own(epack, k, xwin, k, o_sem.at[0, k])

    def m_own(b):
        return own(mpack, b, mwin, b, o_sem.at[1, b])

    def h_own_first(b):
        return own(hpack, b, hwin, b, o_sem.at[2, b])

    def h_own(b):
        return own(hbuf, b, hwin, b + batches, o_sem.at[3, b])

    def start(make, k):
        return lambda index: make(k, index).start()

    def sent(make, k):
        return lambda index: make(k, index).wait_send()

    def landed(make, k):
        return lambda index: make(k, index).wait_recv()

    def begin(b, _):
        each(AROUND, None, start(h_first, b))
        each(AROUND, first, start(m_first, b))
        each(AROUND, first, start(x_first, b))
        each(AROUND, None, start(c_first, b))
        h_own_first(b).start()

        @pl.when(first)
        def _():
            m_own(b).start()
            x_own(b).start()

        return 0

    lax.fori_loop(0, batches, begin, 0)

    def begin_later(k, _):
        each(AROUND, first, start(x_first, k))
        pl.when(first)(lambda: x_own(k).start())
        return 0

    lax.fori_loop(batches, items, begin_later, 0)
    for copy in fetches:
        copy.wait()

    def unpack(window):
        for r in range(wr):
            value = window[r].astype(f32)
            turned = pltpu.roll(value, CH, 1)
            wide[r, pl.ds(SIDE, 16), :] = jnp.where(low, value, turned)
            wide[r, pl.ds(SIDE + 16, 16), :] = jnp.where(low, turned, value)
        for base, column in ((wr, SIDE - EDGE), (wr + 4, SIDE + tc)):
            for slab, (lo, hi) in enumerate(WINDOW_ROWS):
                value = window[base + slab].astype(f32)
                turned = pltpu.roll(value, CH, 1)
                upper = jnp.where(low, value, turned)
                lower = jnp.where(low, turned, value)
                for n in (0, 1):
                    wide[lo[n], pl.ds(column, EDGE), :] = upper[n * EDGE : (n + 1) * EDGE]
                    wide[hi[n], pl.ds(column, EDGE), :] = lower[n * EDGE : (n + 1) * EDGE]

    def spread():
        def tap(r, q):
            return wide[r, pl.ds(SIDE - EDGE - 2 + q, gc), :]

        for r in range(wr):
            taps = [tap(r, q) for q in range(KS)]
            p01[r] = jnp.where(low, taps[0], taps[1]).astype(bf16)
            p23[r] = jnp.where(low, taps[2], taps[3]).astype(bf16)
            p12[r] = jnp.where(low, taps[1], taps[2]).astype(bf16)
            p34[r] = jnp.where(low, taps[3], taps[4]).astype(bf16)
            p40[r] = jnp.where(low, taps[4], tap(min(r + 1, wr - 1), 0)).astype(bf16)

    def patches():
        parts = []
        for p in (0, 2):
            for buffer, at in ((p01, p), (p23, p), (p40, p), (p12, p + 1), (p34, p + 1)):
                parts.append(buffer[at : at + gr].reshape(gr * gc, 128))
        parts.append(p01[4 : 4 + gr].reshape(gr * gc, 128))
        parts.append(p23[4 : 4 + gr].reshape(gr * gc, 128))
        parts.append(p40[4 : 4 + gr].reshape(gr * gc, 128)[:, :CH])
        return jnp.concatenate(parts, axis=1)

    def cell(k, _):
        b = lax.rem(k, batches)
        early = k < batches
        late = k >= batches

        each_source(AROUND, early, landed(h_first, b))
        each_source(AROUND, late, landed(h_next, b))
        pl.when(early)(lambda: h_own_first(b).wait())
        pl.when(late)(lambda: h_own(b).wait())
        unpack(hwin.at[k])
        spread()
        acc_h[...] = dot_last(patches(), wh[...])

        @pl.when(early)
        def _():
            each_source(AROUND, None, landed(c_first, b))
            unpack(cwin.at[b])
            for r in range(gr):
                state[b, r] = wide[r + HALO - 2, pl.ds(SIDE - EDGE, gc), :]
            for r in range(tr):
                state[b, r + 2, pl.ds(EDGE, tc), :] = cel_ref[b, r]

        each_source(AROUND, first & early, landed(m_first, b))
        pl.when(first & early)(lambda: m_own(b).wait())
        each_source(EVERY, jnp.logical_not(first) | late, landed(m_next, k))
        unpack(mwin.at[k])
        spread()
        acc_m[...] = dot_last(patches(), wm[...])
        for r in range(gr):
            memory = wide[r + HALO - 2, pl.ds(SIDE - EDGE, gc), :]
            state[b, r] = jnp.where(low, state[b, r], memory)

        each_source(AROUND, first, landed(x_first, k))
        pl.when(first)(lambda: x_own(k).wait())
        each_source(EVERY, jnp.logical_not(first), landed(x_next, k))
        unpack(xwin.at[k])
        spread()
        acc_x[...] = dot_last(patches(), wx[...])

        grid_col = lax.broadcasted_iota(jnp.int32, (gc, 1), 0) + (col * tc - EDGE)
        col_ok = (grid_col >= 0) & (grid_col < cols * tc)
        for r in range(gr):
            span = slice(r * gc, (r + 1) * gc)
            h0, h1 = acc_h[span, :128], acc_h[span, 128:]
            m0, m1 = acc_m[span, :128], acc_m[span, 128:]
            into = acc_x[span, :128] + jnp.where(low, h0, m0)
            keep = acc_x[span, 128:256] + pltpu.roll(jnp.where(low, m0, h0), CH, 1)
            fresh = acc_x[span, 256:384] + jnp.where(low, h1, m1)
            new = sigmoid(keep + 1.0) * state[b, r] + sigmoid(into) * jnp.tanh(fresh)
            state[b, r] = new
            grid_row = row * tr + (r - 2)
            ok = col_ok & ((grid_row >= 0) & (grid_row < rows * tr))
            joined[r] = jnp.where(ok, new, 0.0)

        def new_memory(r):
            value = state[b, r + 2, pl.ds(EDGE, tc), :]
            return jnp.where(low, pltpu.roll(value, CH, 1), value)

        pack_into(mbuf, k, new_memory)
        each(EVERY, jnp.logical_not(last), start(m_next, k))
        each(EVERY, last & early, start(m_loop, k))

        for q in range(KS):
            for r in range(gr):
                js[q, r] = joined[r, pl.ds(EDGE - 2 + q, tc), :].astype(bf16)
        parts = [
            js[q, 2 * g : 2 * g + tr + 1].reshape((tr + 1) * tc, 128)
            for g in range(3)
            for q in range(KS)
        ]
        out = dot_last(jnp.concatenate(parts, axis=1), wo[...])
        mixed = dot_last(js[2, 2 : 2 + tr].reshape(tr * tc, 128), wmix[...])
        hidden = []
        for r in range(tr):
            grid = slice((r + 2) * gc + EDGE, (r + 2) * gc + EDGE + tc)
            h1 = acc_h[grid, 128:]
            gate = out[r * tc : (r + 1) * tc, :128] + out[(r + 1) * tc : (r + 2) * tc, 128:]
            gate += acc_x[grid, 384:] + jnp.where(low, pltpu.roll(h1, CH, 1), h1)
            hidden.append(sigmoid(gate) * jnp.tanh(mixed[r * tc : (r + 1) * tc]))
        pack_into(hbuf, k, lambda r: hidden[r])
        each(EVERY, jnp.logical_not(last), start(x_next, k))

        @pl.when(early)
        def _():
            each(AROUND, None, start(h_next, k))
            h_own(k).start()

        @pl.when(late)
        def _():
            for r in range(tr):
                outh_ref[b, r] = hidden[r]
            outs_ref[b] = state[b, 2 : 2 + tr, EDGE : EDGE + tc, :]

        return 0

    lax.fori_loop(0, items, cell, 0)

    def finish(k, _):
        each(AROUND, first, sent(x_first, k))
        each(EVERY, jnp.logical_not(last), sent(x_next, k))
        each(EVERY, jnp.logical_not(last), sent(m_next, k))
        return 0

    def finish_early(b, _):
        each(AROUND, first, sent(m_first, b))
        each(EVERY, last, sent(m_loop, b))
        each(AROUND, None, sent(h_first, b))
        each(AROUND, None, sent(h_next, b))
        each(AROUND, None, sent(c_first, b))
        return 0

    lax.fori_loop(0, items, finish, 0)
    lax.fori_loop(0, batches, finish_early, 0)


def per_device(
    sizes,
    frames,
    region_order,
    encoder,
    input_kernel,
    hidden_kernel,
    memory_kernel,
    output_kernel,
    mixing_weight,
    hidden_start,
    cell_start,
    memory_start,
):
    bf16, f32 = jnp.bfloat16, jnp.float32
    sections, rows, cols = sizes
    steps, _, patch, tr, tc = frames.shape
    batches, ch = memory_start.shape[:2]
    items = steps * batches
    gr, gc = tr + 4, tc + 2 * EDGE
    wr, wc = tr + 2 * HALO, tc + 2 * SIDE
    taps = KS * KS * ch

    def twice(value):
        return jnp.concatenate([value, value], -1)

    picked = jnp.take(frames, region_order[:batches], axis=1)
    enc = jnp.einsum(
        "tbcyx,oc->tbyxo", picked, twice(encoder.T).T, preferred_element_type=f32
    )
    enc = enc.astype(bf16).reshape(items, tr, tc, 2 * ch)
    hid = twice(hidden_start[0].transpose(0, 2, 3, 1).astype(bf16))
    cel = twice(cell_start[0].transpose(0, 2, 3, 1))
    mem = twice(memory_start.transpose(0, 2, 3, 1).astype(bf16))

    vmem = pl.BlockSpec(memory_space=pltpu.VMEM)
    anywhere = pl.BlockSpec(memory_space=pl.ANY)
    dma = pltpu.SemaphoreType.DMA
    window, packed = (wr + 8, 16, 128), (tr + 8, 16, 128)
    ends = jax.ShapeDtypeStruct((batches, tr, tc, 2 * ch), f32)
    outh, outs = pl.pallas_call(
        functools.partial(kernel_body, sections, rows, cols, steps, batches),
        out_shape=(ends, ends),
        in_specs=[vmem] * 4 + [anywhere] * 5,
        out_specs=(vmem, vmem),
        scratch_shapes=[
            pltpu.VMEM((items,) + window, bf16),
            pltpu.VMEM((items,) + window, bf16),
            pltpu.VMEM((items,) + window, bf16),
            pltpu.VMEM((batches,) + window, bf16),
            pltpu.VMEM((items,) + packed, bf16),
            pltpu.VMEM((batches,) + packed, bf16),
            pltpu.VMEM((batches,) + packed, bf16),
            pltpu.VMEM((batches,) + packed, bf16),
            pltpu.VMEM((items,) + packed, bf16),
            pltpu.VMEM((items,) + packed, bf16),
            pltpu.VMEM((wr, wc, 128), f32),
        ]
        + [pltpu.VMEM((wr, gc, 128), bf16)] * 5
        + [
            pltpu.VMEM((gr * gc, 512), f32),
            pltpu.VMEM((gr * gc, 256), f32),
            pltpu.VMEM((gr * gc, 256), f32),
            pltpu.VMEM((batches, gr, gc, 128), f32),
            pltpu.VMEM((gr, gc, 128), f32),
            pltpu.VMEM((KS, gr + 1, tc, 128), bf16),
            pltpu.VMEM((8 * ch, taps), bf16),
            pltpu.VMEM((4 * ch, taps), bf16),
            pltpu.VMEM((4 * ch, taps), bf16),
            pltpu.VMEM((4 * ch, 3 * KS * 2 * ch), bf16),
            pltpu.VMEM((2 * ch, 2 * ch), bf16),
            dma((24,)),
            dma((items, 9)),
            dma((batches, 9)),
            dma((batches, 9)),
            dma((items, 9)),
            dma((items, 9)),
            dma((items, 9)),
            dma((items, 9)),
            dma((batches, 9)),
            dma((items, 9)),
            dma((batches, 9)),
            dma((batches, 9)),
            dma((4, items)),
        ],
        compiler_params=pltpu.CompilerParams(
            collective_id=0, has_side_effects=True, vmem_limit_bytes=48 << 20
        ),
        name="predrnn",
    )(
        enc,
        hid,
        cel,
        mem,
        input_kernel[0],
        hidden_kernel[0],
        memory_kernel[0],
        output_kernel[0],
        mixing_weight[0],
    )

    def back(value):
        return value.transpose(0, 3, 1, 2)[None]

    return back(outh[..., :ch]), back(outs[..., :ch]), back(outs[..., ch:])


def solution(mesh):
    sizes = tuple(mesh.shape[name] for name in ("section", "row", "col"))
    return jax.shard_map(
        functools.partial(per_device, sizes),
        mesh=mesh,
        in_specs=(
            P(None, None, None, "row", "col"),
            P(),
            P(),
            P("section", None, None),
            P("section", None, None),
            P("section", None, None),
            P("section", None, None),
            P("section", None, None),
            P("section", None, None, "row", "col"),
            P("section", None, None, "row", "col"),
            P(None, None, "row", "col"),
        ),
        out_specs=(
            P("section", None, None, "row", "col"),
            P("section", None, None, "row", "col"),
            P("section", None, None, "row", "col"),
        ),
        check_vma=False,
    )
```

```python
import functools

import jax
import jax.numpy as jnp
from jax import lax
from jax.experimental import pallas as pl
from jax.experimental.pallas import tpu as pltpu
from jax.sharding import PartitionSpec as P

KS = 5
HALO = 4
SIDE = 16
EDGE = 8
CH = 64
DIRS = [(-1, -1), (-1, 1), (1, -1), (1, 1), (0, -1), (0, 1), (-1, 0), (1, 0), (0, 0)]
AROUND = list(range(8))
EVERY = list(range(9))
MESH = pl.DeviceIdType.MESH

SLABS = {
    (0, 0): (0, 4, 8),
    (1, 0): (4, 0, 4),
    (-1, 0): (0, 12, 4),
    (0, 1): (13, 17, 2),
    (1, 1): (15, 16, 1),
    (-1, 1): (12, 19, 1),
    (0, -1): (9, 21, 2),
    (1, -1): (11, 20, 1),
    (-1, -1): (8, 23, 1),
}
STRIP_ROWS = [((0, 1), (2, 3)), ((0, 1), (4, 5)), ((2, 3), (6, 7)), ((4, 5), (6, 7))]
WINDOW_ROWS = [((0, 1), (2, 3)), ((4, 5), (8, 9)), ((6, 7), (10, 11)), ((12, 13), (14, 15))]


def sigmoid(value):
    return 0.5 * jnp.tanh(0.5 * value) + 0.5


def dot_last(left, right):
    def part(a, b):
        return lax.dot_general(a, b, (((1,), (1,)), ((), ())), preferred_element_type=jnp.float32)

    if left.shape[1] < 1600:
        return part(left, right)
    return jnp.concatenate([part(left[:288], right), part(left[288:], right)], 0)


def kernel_body(
    sections,
    rows,
    cols,
    steps,
    batches,
    enc_in,
    hid_in,
    cel_in,
    mem_in,
    ik_ref,
    hk_ref,
    mk_ref,
    ok_ref,
    mix_ref,
    outh_ref,
    outs_ref,
    xwin,
    mwin,
    hwin,
    cwin,
    epack,
    hpack,
    cpack,
    mpack,
    hbuf,
    mbuf,
    wide,
    p01,
    p23,
    p40,
    p12,
    p34,
    acc_h,
    acc_m,
    state,
    memory,
    fresh_memory,
    joined,
    js,
    enc_ref,
    hid_ref,
    cel_ref,
    mem_ref,
    wxm,
    wxc,
    wh,
    wm,
    wo,
    wmix,
    w_sem,
    e_send,
    f_send,
    i_send,
    x_send,
    x_recv,
    m_send,
    m_recv,
    h_send,
    h_recv,
    c_send,
    c_recv,
    o_sem,
):
    bf16, f32 = jnp.bfloat16, jnp.float32
    sec = lax.axis_index("section")
    row = lax.axis_index("row")
    col = lax.axis_index("col")
    tr, tc = enc_in.shape[1], enc_in.shape[2]
    gr, gc = tr + 4, tc + 2 * EDGE
    wr = tr + 2 * HALO
    items = steps * batches
    first = sec == 0
    last = sec == sections - 1
    after = lax.rem(sec + 1, sections)
    before = lax.rem(sec + sections - 1, sections)

    half = KS * 2 * CH
    fetches = []

    def fetch(source, target):
        copy = pltpu.make_async_copy(source, target, w_sem.at[len(fetches)])
        copy.start()
        fetches.append(copy)
        return copy

    in_hid = fetch(hid_in, hid_ref)
    in_mem = fetch(mem_in, mem_ref)
    in_enc = fetch(enc_in, enc_ref)
    in_cel = fetch(cel_in, cel_ref)
    in_wh = [fetch(hk_ref, wh)]
    in_wm = [fetch(mk_ref, wm.at[pl.ds(0, 3 * CH)])]
    in_wxm = [fetch(ik_ref.at[pl.ds(3 * CH, 3 * CH)], wxm.at[pl.ds(0, 3 * CH)])]
    in_wxc = [
        fetch(ik_ref.at[pl.ds(0, 3 * CH)], wxc.at[pl.ds(0, 3 * CH)]),
        fetch(ik_ref.at[pl.ds(6 * CH, CH)], wxc.at[pl.ds(3 * CH, CH)]),
    ]
    in_wo = [
        fetch(
            ok_ref.at[:, pl.ds(p * half, half)],
            wo.at[pl.ds(p % 4 * CH, CH), pl.ds(p // 4 * half, half)],
        )
        for p in range(KS)
    ]
    in_wo += [fetch(mix_ref, wmix.at[pl.ds(copy * CH, CH)]) for copy in (0, 1)]

    def exists(dr, dc):
        found = None
        for ok in (
            row > 0 if dr < 0 else row < rows - 1 if dr > 0 else None,
            col > 0 if dc < 0 else col < cols - 1 if dc > 0 else None,
        ):
            if ok is not None:
                found = ok if found is None else found & ok
        return found

    def guarded(cond, fn):
        if cond is None:
            fn()
        else:
            pl.when(cond)(fn)

    def both(a, b):
        return b if a is None else a if b is None else a & b

    def copy_of(src, src_item, dst, dst_item, send_sem, recv_sem, target, index):
        dr, dc = DIRS[index]
        from_slab, to_slab, count = SLABS[(dr, dc)]
        return pltpu.make_async_remote_copy(
            src_ref=src.at[src_item, pl.ds(from_slab, count)],
            dst_ref=dst.at[dst_item, pl.ds(to_slab, count)],
            send_sem=send_sem.at[src_item, index],
            recv_sem=recv_sem.at[dst_item, index],
            device_id={
                "section": target,
                "row": lax.rem(row + dr + rows, rows),
                "col": lax.rem(col + dc + cols, cols),
            },
            device_id_type=MESH,
        )

    def each(indices, cond, fn):
        for index in indices:
            guarded(both(cond, exists(*DIRS[index])), functools.partial(fn, index))

    def each_source(indices, cond, fn):
        for index in indices:
            dr, dc = DIRS[index]
            guarded(both(cond, exists(-dr, -dc)), functools.partial(fn, index))

    def clear(k, _):
        zero = jnp.zeros(xwin.shape[1:], bf16)
        xwin[k] = zero
        mwin[k] = zero
        hwin[k] = zero
        return 0

    lax.fori_loop(0, items, clear, 0)

    def clear_cells(b, _):
        cwin[b] = jnp.zeros(cwin.shape[1:], bf16)
        return 0

    lax.fori_loop(0, batches, clear_cells, 0)

    barrier = pltpu.get_barrier_semaphore()
    for index in EVERY:
        dr, dc = DIRS[index]

        def greet(dr=dr, dc=dc):
            for target in (after, before) + (() if (dr, dc) == (0, 0) else (sec,)):
                pl.semaphore_signal(
                    barrier,
                    inc=1,
                    device_id={"section": target, "row": row + dr, "col": col + dc},
                    device_id_type=MESH,
                )

        guarded(exists(dr, dc), greet)

    js[:, gr:] = jnp.zeros((KS, 3, tc, 128), bf16)
    wide[...] = jnp.zeros(wide.shape, f32)
    for target in (wm, wxm):
        target[3 * CH :, :] = jnp.zeros((CH, target.shape[1]), bf16)
    wo[CH:, half:] = jnp.zeros((3 * CH, half), bf16)

    low = lax.broadcasted_iota(jnp.int32, (1, 128), 1) < CH

    def turn(value):
        return pltpu.roll(value, CH, 1)

    def pack_into(target, item, value_of, merge):
        line = [value_of(r) for r in range(tr)]
        for r in range(tr):
            target[item, r] = merge(line[r][:16], line[r][16:32]).astype(bf16)
        for side, begin in ((8, 0), (12, tc - EDGE)):
            strip = [part[begin : begin + EDGE] for part in line]
            for slab, (lo, hi) in enumerate(STRIP_ROWS):
                upper = jnp.concatenate([strip[lo[0]], strip[lo[1]]], 0)
                lower = jnp.concatenate([strip[hi[0]], strip[hi[1]]], 0)
                target[item, side + slab] = merge(upper, lower).astype(bf16)

    def merge_alike(one, two):
        return jnp.where(low, one, two)

    def merge_low(one, two):
        return jnp.where(low, one, turn(two))

    def merge_high(one, two):
        return jnp.where(low, turn(one), two)

    def pack_first(b, _):
        pack_into(hpack, b, lambda r: hid_ref[b, r].astype(f32), merge_alike)
        pack_into(mpack, b, lambda r: mem_ref[b, r].astype(f32), merge_alike)
        pack_into(cpack, b, lambda r: cel_ref[b, r], merge_alike)
        return 0

    for copy in (in_hid, in_mem, in_cel, in_enc):
        copy.wait()
    lax.fori_loop(0, batches, pack_first, 0)

    def pack_inputs(k, _):
        pack_into(epack, k, lambda r: enc_ref[k, r].astype(f32), merge_alike)
        return 0

    lax.fori_loop(0, items, pack_inputs, 0)

    near_rows = 1 + (row > 0).astype(jnp.int32) + (row < rows - 1).astype(jnp.int32)
    near_cols = 1 + (col > 0).astype(jnp.int32) + (col < cols - 1).astype(jnp.int32)
    pl.semaphore_wait(barrier, 3 * near_rows * near_cols - 1)

    def x_first(k, index):
        return copy_of(epack, k, xwin, k, e_send, x_recv, sec, index)

    def m_first(b, index):
        return copy_of(mpack, b, mwin, b, f_send, m_recv, sec, index)

    def h_first(b, index):
        return copy_of(hpack, b, hwin, b, i_send, h_recv, sec, index)

    def c_first(b, index):
        return copy_of(cpack, b, cwin, b, c_send, c_recv, sec, index)

    def x_next(k, index):
        return copy_of(hbuf, k, xwin, k, x_send, x_recv, after, index)

    def m_next(k, index):
        return copy_of(mbuf, k, mwin, k, m_send, m_recv, after, index)

    def m_loop(k, index):
        return copy_of(mbuf, k, mwin, k + batches, m_send, m_recv, after, index)

    def h_next(k, index):
        return copy_of(hbuf, k, hwin, k + batches, h_send, h_recv, sec, index)

    def own(src, src_item, dst, dst_item, sem):
        return pltpu.make_async_copy(
            src.at[src_item, pl.ds(0, tr)], dst.at[dst_item, pl.ds(HALO, tr)], sem
        )

    def x_own(k):
        return own(epack, k, xwin, k, o_sem.at[0, k])

    def m_own(b):
        return own(mpack, b, mwin, b, o_sem.at[1, b])

    def h_own_first(b):
        return own(hpack, b, hwin, b, o_sem.at[2, b])

    def h_own(b):
        return own(hbuf, b, hwin, b + batches, o_sem.at[3, b])

    def start(make, k):
        return lambda index: make(k, index).start()

    def sent(make, k):
        return lambda index: make(k, index).wait_send()

    def landed(make, k):
        return lambda index: make(k, index).wait_recv()

    def begin(b, _):
        each(AROUND, None, start(h_first, b))
        each(AROUND, first, start(m_first, b))
        each(AROUND, first, start(x_first, b))
        each(AROUND, None, start(c_first, b))
        h_own_first(b).start()

        @pl.when(first)
        def _():
            m_own(b).start()
            x_own(b).start()

        return 0

    lax.fori_loop(0, batches, begin, 0)

    def begin_later(k, _):
        each(AROUND, first, start(x_first, k))
        pl.when(first)(lambda: x_own(k).start())
        return 0

    lax.fori_loop(batches, items, begin_later, 0)
    def unpack(window):
        for r in range(wr):
            value = window[r].astype(f32)
            turned = pltpu.roll(value, CH, 1)
            wide[r, pl.ds(SIDE, 16), :] = jnp.where(low, value, turned)
            wide[r, pl.ds(SIDE + 16, 16), :] = jnp.where(low, turned, value)
        for base, column in ((wr, SIDE - EDGE), (wr + 4, SIDE + tc)):
            for slab, (lo, hi) in enumerate(WINDOW_ROWS):
                value = window[base + slab].astype(f32)
                turned = pltpu.roll(value, CH, 1)
                upper = jnp.where(low, value, turned)
                lower = jnp.where(low, turned, value)
                for n in (0, 1):
                    wide[lo[n], pl.ds(column, EDGE), :] = upper[n * EDGE : (n + 1) * EDGE]
                    wide[hi[n], pl.ds(column, EDGE), :] = lower[n * EDGE : (n + 1) * EDGE]

    def spread():
        def tap(r, q):
            return wide[r, pl.ds(SIDE - EDGE - 2 + q, gc), :]

        for r in range(wr):
            taps = [tap(r, q) for q in range(KS)]
            p01[r] = jnp.where(low, taps[0], taps[1]).astype(bf16)
            p23[r] = jnp.where(low, taps[2], taps[3]).astype(bf16)
            p12[r] = jnp.where(low, taps[1], taps[2]).astype(bf16)
            p34[r] = jnp.where(low, taps[3], taps[4]).astype(bf16)
            p40[r] = jnp.where(low, taps[4], tap(min(r + 1, wr - 1), 0)).astype(bf16)

    def patches():
        parts = []
        for p in (0, 2):
            for buffer, at in ((p01, p), (p23, p), (p40, p), (p12, p + 1), (p34, p + 1)):
                parts.append(buffer[at : at + gr].reshape(gr * gc, 128))
        parts.append(p01[4 : 4 + gr].reshape(gr * gc, 128))
        parts.append(p23[4 : 4 + gr].reshape(gr * gc, 128))
        parts.append(p40[4 : 4 + gr].reshape(gr * gc, 128)[:, :CH])
        return jnp.concatenate(parts, axis=1)

    def arrived(k, copies):
        @pl.when(k == 0)
        def _():
            for copy in copies:
                copy.wait()

    bias = jnp.where(low, 0.0, 1.0)

    def cell(k, _):
        b = lax.rem(k, batches)
        early = k < batches
        late = k >= batches

        each_source(AROUND, early, landed(h_first, b))
        each_source(AROUND, late, landed(h_next, b))
        pl.when(early)(lambda: h_own_first(b).wait())
        pl.when(late)(lambda: h_own(b).wait())
        arrived(k, in_wh)
        unpack(hwin.at[k])
        spread()
        acc_h[...] = dot_last(patches(), wh[...])

        @pl.when(early)
        def _():
            each_source(AROUND, None, landed(c_first, b))
            unpack(cwin.at[b])
            for r in range(gr):
                state[b, r] = wide[r + HALO - 2, pl.ds(SIDE - EDGE, gc), :]
            for r in range(tr):
                state[b, r + 2, pl.ds(EDGE, tc), :] = cel_ref[b, r]

        each_source(AROUND, first & early, landed(m_first, b))
        pl.when(first & early)(lambda: m_own(b).wait())
        each_source(EVERY, jnp.logical_not(first) | late, landed(m_next, k))
        arrived(k, in_wm)
        unpack(mwin.at[k])
        spread()
        acc_m[...] = dot_last(patches(), wm[...])
        for r in range(gr):
            memory[r] = wide[r + HALO - 2, pl.ds(SIDE - EDGE, gc), :]

        each_source(AROUND, first, landed(x_first, k))
        pl.when(first)(lambda: x_own(k).wait())
        each_source(EVERY, jnp.logical_not(first), landed(x_next, k))
        arrived(k, in_wxm + in_wxc)
        unpack(xwin.at[k])
        spread()
        acc_m[...] += dot_last(patches(), wxm[...])
        acc_h[...] += dot_last(patches(), wxc[...])

        for r in range(gr):
            span = slice(r * gc, (r + 1) * gc)
            gates = sigmoid(acc_m[span, :128] + bias)
            fresh_memory[r] = turn(gates) * memory[r] + gates * jnp.tanh(acc_m[span, 128:])
        pack_into(mbuf, k, lambda r: fresh_memory[r + 2, pl.ds(EDGE, tc), :], merge_low)
        each(EVERY, jnp.logical_not(last), start(m_next, k))
        each(EVERY, last & early, start(m_loop, k))

        grid_col = lax.broadcasted_iota(jnp.int32, (gc, 1), 0) + (col * tc - EDGE)
        col_ok = (grid_col >= 0) & (grid_col < cols * tc)
        for r in range(gr):
            span = slice(r * gc, (r + 1) * gc)
            gates = sigmoid(acc_h[span, :128] + bias)
            new = turn(gates) * state[b, r] + gates * jnp.tanh(acc_h[span, 128:])
            state[b, r] = new
            grid_row = row * tr + (r - 2)
            ok = col_ok & ((grid_row >= 0) & (grid_row < rows * tr))
            joined[r] = jnp.where(ok, jnp.where(low, new, turn(fresh_memory[r])), 0.0)

        arrived(k, in_wo)
        for q in range(KS):
            for r in range(gr):
                js[q, r] = joined[r, pl.ds(EDGE - 2 + q, tc), :].astype(bf16)
        parts = [
            js[q, 4 * g : 4 * g + tr + 3].reshape((tr + 3) * tc, 128)
            for g in range(2)
            for q in range(KS)
        ]
        out = dot_last(jnp.concatenate(parts, axis=1), wo[...])
        mixed = dot_last(js[2, 2 : 2 + tr].reshape(tr * tc, 128), wmix[...])
        hidden = []
        for r in range(tr):
            grid = slice((r + 2) * gc + EDGE, (r + 2) * gc + EDGE + tc)
            line = [slice((r + n) * tc, (r + n + 1) * tc) for n in range(4)]
            gate = out[line[1], :128] + out[line[3], 128:] + acc_h[grid, 128:]
            gate += turn(out[line[0], :128] + out[line[2], 128:])
            hidden.append(sigmoid(gate) * jnp.tanh(mixed[r * tc : (r + 1) * tc]))
        pack_into(hbuf, k, lambda r: hidden[r], merge_high)
        each(EVERY, jnp.logical_not(last), start(x_next, k))

        @pl.when(early)
        def _():
            each(AROUND, None, start(h_next, k))
            h_own(k).start()

        @pl.when(late)
        def _():
            for r in range(tr):
                outh_ref[b, r] = hidden[r]
            outs_ref[b] = joined[2 : 2 + tr, EDGE : EDGE + tc, :]

        return 0

    lax.fori_loop(0, items, cell, 0)

    def finish(k, _):
        each(AROUND, first, sent(x_first, k))
        each(EVERY, jnp.logical_not(last), sent(x_next, k))
        each(EVERY, jnp.logical_not(last), sent(m_next, k))
        return 0

    def finish_early(b, _):
        each(AROUND, first, sent(m_first, b))
        each(EVERY, last, sent(m_loop, b))
        each(AROUND, None, sent(h_first, b))
        each(AROUND, None, sent(h_next, b))
        each(AROUND, None, sent(c_first, b))
        return 0

    lax.fori_loop(0, items, finish, 0)
    lax.fori_loop(0, batches, finish_early, 0)


def per_device(
    sizes,
    frames,
    region_order,
    encoder,
    input_kernel,
    hidden_kernel,
    memory_kernel,
    output_kernel,
    mixing_weight,
    hidden_start,
    cell_start,
    memory_start,
):
    bf16, f32 = jnp.bfloat16, jnp.float32
    sections, rows, cols = sizes
    steps, _, patch, tr, tc = frames.shape
    batches, ch = memory_start.shape[:2]
    items = steps * batches
    gr, gc = tr + 4, tc + 2 * EDGE
    wr, wc = tr + 2 * HALO, tc + 2 * SIDE
    taps = KS * KS * ch

    def twice(value):
        return jnp.concatenate([value, value], -1)

    picked = jnp.take(frames, region_order[:batches], axis=1)
    enc = jnp.einsum(
        "tbcyx,oc->tbyxo", picked, twice(encoder.T).T, preferred_element_type=f32
    )
    enc = enc.astype(bf16).reshape(items, tr, tc, 2 * ch)
    hid = twice(hidden_start[0].transpose(0, 2, 3, 1).astype(bf16))
    cel = twice(cell_start[0].transpose(0, 2, 3, 1))
    mem = twice(memory_start.transpose(0, 2, 3, 1).astype(bf16))

    vmem = pl.BlockSpec(memory_space=pltpu.VMEM)
    anywhere = pl.BlockSpec(memory_space=pl.ANY)
    dma = pltpu.SemaphoreType.DMA
    window, packed = (wr + 8, 16, 128), (tr + 8, 16, 128)
    ends = jax.ShapeDtypeStruct((batches, tr, tc, 2 * ch), f32)
    outh, outs = pl.pallas_call(
        functools.partial(kernel_body, sections, rows, cols, steps, batches),
        out_shape=(ends, ends),
        in_specs=[anywhere] * 9,
        out_specs=(vmem, vmem),
        scratch_shapes=[
            pltpu.VMEM((items,) + window, bf16),
            pltpu.VMEM((items,) + window, bf16),
            pltpu.VMEM((items,) + window, bf16),
            pltpu.VMEM((batches,) + window, bf16),
            pltpu.VMEM((items,) + packed, bf16),
            pltpu.VMEM((batches,) + packed, bf16),
            pltpu.VMEM((batches,) + packed, bf16),
            pltpu.VMEM((batches,) + packed, bf16),
            pltpu.VMEM((items,) + packed, bf16),
            pltpu.VMEM((items,) + packed, bf16),
            pltpu.VMEM((wr, wc, 128), f32),
        ]
        + [pltpu.VMEM((wr, gc, 128), bf16)] * 5
        + [
            pltpu.VMEM((gr * gc, 256), f32),
            pltpu.VMEM((gr * gc, 256), f32),
            pltpu.VMEM((batches, gr, gc, 128), f32),
            pltpu.VMEM((gr, gc, 128), f32),
            pltpu.VMEM((gr, gc, 128), f32),
            pltpu.VMEM((gr, gc, 128), f32),
            pltpu.VMEM((KS, gr + 3, tc, 128), bf16),
            pltpu.VMEM(enc.shape, bf16),
            pltpu.VMEM(hid.shape, bf16),
            pltpu.VMEM(cel.shape, f32),
            pltpu.VMEM(mem.shape, bf16),
            pltpu.VMEM((4 * ch, taps), bf16),
            pltpu.VMEM((4 * ch, taps), bf16),
            pltpu.VMEM((4 * ch, taps), bf16),
            pltpu.VMEM((4 * ch, taps), bf16),
            pltpu.VMEM((4 * ch, 2 * KS * 2 * ch), bf16),
            pltpu.VMEM((2 * ch, 2 * ch), bf16),
            dma((24,)),
            dma((items, 9)),
            dma((batches, 9)),
            dma((batches, 9)),
            dma((items, 9)),
            dma((items, 9)),
            dma((items, 9)),
            dma((items, 9)),
            dma((batches, 9)),
            dma((items, 9)),
            dma((batches, 9)),
            dma((batches, 9)),
            dma((4, items)),
        ],
        compiler_params=pltpu.CompilerParams(
            collective_id=0, has_side_effects=True, vmem_limit_bytes=48 << 20
        ),
        name="predrnn",
    )(
        enc,
        hid,
        cel,
        mem,
        input_kernel[0],
        hidden_kernel[0],
        memory_kernel[0],
        output_kernel[0],
        mixing_weight[0],
    )

    def back(value):
        return value.transpose(0, 3, 1, 2)[None]

    return back(outh[..., ch:]), back(outs[..., :ch]), back(outs[..., ch:])


def solution(mesh):
    sizes = tuple(mesh.shape[name] for name in ("section", "row", "col"))
    return jax.shard_map(
        functools.partial(per_device, sizes),
        mesh=mesh,
        in_specs=(
            P(None, None, None, "row", "col"),
            P(),
            P(),
            P("section", None, None),
            P("section", None, None),
            P("section", None, None),
            P("section", None, None),
            P("section", None, None),
            P("section", None, None, "row", "col"),
            P("section", None, None, "row", "col"),
            P(None, None, "row", "col"),
        ),
        out_specs=(
            P("section", None, None, "row", "col"),
            P("section", None, None, "row", "col"),
            P("section", None, None, "row", "col"),
        ),
        check_vma=False,
    )
```

```python
import functools

import jax
import jax.numpy as jnp
from jax import lax
from jax.experimental import pallas as pl
from jax.experimental.pallas import tpu as pltpu
from jax.sharding import PartitionSpec as P

KS = 5
HALO = 4
SIDE = 16
EDGE = 8
CH = 64
DIRS = [(-1, -1), (-1, 1), (1, -1), (1, 1), (0, -1), (0, 1), (-1, 0), (1, 0), (0, 0)]
AROUND = list(range(8))
EVERY = list(range(9))
MESH = pl.DeviceIdType.MESH

SLABS = {
    (0, 0): (0, 4, 8),
    (1, 0): (4, 0, 4),
    (-1, 0): (0, 12, 4),
    (0, 1): (13, 17, 2),
    (1, 1): (15, 16, 1),
    (-1, 1): (12, 19, 1),
    (0, -1): (9, 21, 2),
    (1, -1): (11, 20, 1),
    (-1, -1): (8, 23, 1),
}
STRIP_ROWS = [((0, 1), (2, 3)), ((0, 1), (4, 5)), ((2, 3), (6, 7)), ((4, 5), (6, 7))]
WINDOW_ROWS = [((0, 1), (2, 3)), ((4, 5), (8, 9)), ((6, 7), (10, 11)), ((12, 13), (14, 15))]


def sigmoid(value):
    return 0.5 * jnp.tanh(0.5 * value) + 0.5


def dot_last(left, right):
    def part(a, b):
        return lax.dot_general(a, b, (((1,), (1,)), ((), ())), preferred_element_type=jnp.float32)

    if left.shape[1] < 1600:
        return part(left, right)
    return jnp.concatenate([part(left[:288], right), part(left[288:], right)], 0)


def dot_rows(left, right):
    half = left.shape[0] // 2
    return jnp.concatenate(
        [
            jnp.dot(part, right, preferred_element_type=jnp.float32)
            for part in (left[:half], left[half:])
        ],
        0,
    )


def kernel_body(
    sections,
    rows,
    cols,
    steps,
    batches,
    enc_in,
    hid_in,
    cel_in,
    mem_in,
    ik_ref,
    hk_ref,
    mk_ref,
    ok_ref,
    mix_ref,
    outh_ref,
    outs_ref,
    xwin,
    mwin,
    hwin,
    cwin,
    epack,
    hpack,
    cpack,
    mpack,
    hbuf,
    mbuf,
    wide,
    p01,
    p23,
    p40,
    p12,
    p34,
    acc_h,
    acc_m,
    state,
    memory,
    fresh_memory,
    joined,
    js,
    enc_ref,
    hid_ref,
    cel_ref,
    mem_ref,
    wxm,
    wxc,
    wh,
    wm,
    wo,
    wmix,
    w_sem,
    e_send,
    f_send,
    i_send,
    x_send,
    x_recv,
    m_send,
    m_recv,
    h_send,
    h_recv,
    c_send,
    c_recv,
    o_sem,
):
    bf16, f32 = jnp.bfloat16, jnp.float32
    sec = lax.axis_index("section")
    row = lax.axis_index("row")
    col = lax.axis_index("col")
    tr, tc = enc_in.shape[1], enc_in.shape[2]
    gr, gc = tr + 4, tc + 2 * EDGE
    wr = tr + 2 * HALO
    items = steps * batches
    first = sec == 0
    last = sec == sections - 1
    after = lax.rem(sec + 1, sections)
    before = lax.rem(sec + sections - 1, sections)

    half = KS * 2 * CH
    fetches = []

    def fetch(source, target):
        copy = pltpu.make_async_copy(source, target, w_sem.at[len(fetches)])
        copy.start()
        fetches.append(copy)
        return copy

    in_hid = fetch(hid_in, hid_ref)
    in_mem = fetch(mem_in, mem_ref)
    in_enc = fetch(enc_in, enc_ref)
    in_cel = fetch(cel_in, cel_ref)
    in_wh = [fetch(hk_ref, wh)]
    in_wm = [fetch(mk_ref, wm.at[pl.ds(0, 3 * CH)])]
    in_wxm = [fetch(ik_ref.at[pl.ds(3 * CH, 3 * CH)], wxm.at[pl.ds(0, 3 * CH)])]
    in_wxc = [
        fetch(ik_ref.at[pl.ds(0, 3 * CH)], wxc.at[pl.ds(0, 3 * CH)]),
        fetch(ik_ref.at[pl.ds(6 * CH, CH)], wxc.at[pl.ds(3 * CH, CH)]),
    ]
    in_wo = [
        fetch(
            ok_ref.at[:, pl.ds(p * half, half)],
            wo.at[pl.ds(p % 4 * CH, CH), pl.ds(p // 4 * half, half)],
        )
        for p in range(KS)
    ]
    in_wo += [fetch(mix_ref, wmix.at[pl.ds(copy * CH, CH)]) for copy in (0, 1)]

    def exists(dr, dc):
        found = None
        for ok in (
            row > 0 if dr < 0 else row < rows - 1 if dr > 0 else None,
            col > 0 if dc < 0 else col < cols - 1 if dc > 0 else None,
        ):
            if ok is not None:
                found = ok if found is None else found & ok
        return found

    def guarded(cond, fn):
        if cond is None:
            fn()
        else:
            pl.when(cond)(fn)

    def both(a, b):
        return b if a is None else a if b is None else a & b

    def copy_of(src, src_item, dst, dst_item, send_sem, recv_sem, target, index):
        dr, dc = DIRS[index]
        from_slab, to_slab, count = SLABS[(dr, dc)]
        return pltpu.make_async_remote_copy(
            src_ref=src.at[src_item, pl.ds(from_slab, count)],
            dst_ref=dst.at[dst_item, pl.ds(to_slab, count)],
            send_sem=send_sem.at[src_item, index],
            recv_sem=recv_sem.at[dst_item, index],
            device_id={
                "section": target,
                "row": lax.rem(row + dr + rows, rows),
                "col": lax.rem(col + dc + cols, cols),
            },
            device_id_type=MESH,
        )

    def each(indices, cond, fn):
        for index in indices:
            guarded(both(cond, exists(*DIRS[index])), functools.partial(fn, index))

    def each_source(indices, cond, fn):
        for index in indices:
            dr, dc = DIRS[index]
            guarded(both(cond, exists(-dr, -dc)), functools.partial(fn, index))

    def clear(k, _):
        zero = jnp.zeros(xwin.shape[1:], bf16)
        xwin[k] = zero
        mwin[k] = zero
        hwin[k] = zero
        return 0

    lax.fori_loop(0, items, clear, 0)

    def clear_cells(b, _):
        cwin[b] = jnp.zeros(cwin.shape[1:], bf16)
        return 0

    lax.fori_loop(0, batches, clear_cells, 0)

    barrier = pltpu.get_barrier_semaphore()
    for index in EVERY:
        dr, dc = DIRS[index]

        def greet(dr=dr, dc=dc):
            for target in (after, before) + (() if (dr, dc) == (0, 0) else (sec,)):
                pl.semaphore_signal(
                    barrier,
                    inc=1,
                    device_id={"section": target, "row": row + dr, "col": col + dc},
                    device_id_type=MESH,
                )

        guarded(exists(dr, dc), greet)

    js[:, gr:] = jnp.zeros((KS, 3, tc, 128), bf16)
    wide[...] = jnp.zeros(wide.shape, f32)
    for target in (wm, wxm):
        target[3 * CH :, :] = jnp.zeros((CH, target.shape[1]), bf16)
    wo[CH:, half:] = jnp.zeros((3 * CH, half), bf16)

    low = lax.broadcasted_iota(jnp.int32, (1, 128), 1) < CH

    def turn(value):
        return pltpu.roll(value, CH, 1)

    def pack_into(target, item, value_of, merge):
        line = [value_of(r) for r in range(tr)]
        for r in range(tr):
            target[item, r] = merge(line[r][:16], line[r][16:32]).astype(bf16)
        for side, begin in ((8, 0), (12, tc - EDGE)):
            strip = [part[begin : begin + EDGE] for part in line]
            for slab, (lo, hi) in enumerate(STRIP_ROWS):
                upper = jnp.concatenate([strip[lo[0]], strip[lo[1]]], 0)
                lower = jnp.concatenate([strip[hi[0]], strip[hi[1]]], 0)
                target[item, side + slab] = merge(upper, lower).astype(bf16)

    def merge_alike(one, two):
        return jnp.where(low, one, two)

    def merge_low(one, two):
        return jnp.where(low, one, turn(two))

    def merge_high(one, two):
        return jnp.where(low, turn(one), two)

    def pack_first(b, _):
        pack_into(hpack, b, lambda r: hid_ref[b, r].astype(f32), merge_alike)
        pack_into(mpack, b, lambda r: mem_ref[b, r].astype(f32), merge_alike)
        pack_into(cpack, b, lambda r: cel_ref[b, r], merge_alike)
        return 0

    for copy in (in_hid, in_mem, in_cel, in_enc):
        copy.wait()
    lax.fori_loop(0, batches, pack_first, 0)

    def pack_inputs(k, _):
        pack_into(epack, k, lambda r: enc_ref[k, r].astype(f32), merge_alike)
        return 0

    lax.fori_loop(0, items, pack_inputs, 0)

    near_rows = 1 + (row > 0).astype(jnp.int32) + (row < rows - 1).astype(jnp.int32)
    near_cols = 1 + (col > 0).astype(jnp.int32) + (col < cols - 1).astype(jnp.int32)
    pl.semaphore_wait(barrier, 3 * near_rows * near_cols - 1)

    def x_first(k, index):
        return copy_of(epack, k, xwin, k, e_send, x_recv, sec, index)

    def m_first(b, index):
        return copy_of(mpack, b, mwin, b, f_send, m_recv, sec, index)

    def h_first(b, index):
        return copy_of(hpack, b, hwin, b, i_send, h_recv, sec, index)

    def c_first(b, index):
        return copy_of(cpack, b, cwin, b, c_send, c_recv, sec, index)

    def x_next(k, index):
        return copy_of(hbuf, k, xwin, k, x_send, x_recv, after, index)

    def m_next(k, index):
        return copy_of(mbuf, k, mwin, k, m_send, m_recv, after, index)

    def m_loop(k, index):
        return copy_of(mbuf, k, mwin, k + batches, m_send, m_recv, after, index)

    def h_next(k, index):
        return copy_of(hbuf, k, hwin, k + batches, h_send, h_recv, sec, index)

    def own(src, src_item, dst, dst_item, sem):
        return pltpu.make_async_copy(
            src.at[src_item, pl.ds(0, tr)], dst.at[dst_item, pl.ds(HALO, tr)], sem
        )

    def x_own(k):
        return own(epack, k, xwin, k, o_sem.at[0, k])

    def m_own(b):
        return own(mpack, b, mwin, b, o_sem.at[1, b])

    def h_own_first(b):
        return own(hpack, b, hwin, b, o_sem.at[2, b])

    def h_own(b):
        return own(hbuf, b, hwin, b + batches, o_sem.at[3, b])

    def start(make, k):
        return lambda index: make(k, index).start()

    def sent(make, k):
        return lambda index: make(k, index).wait_send()

    def landed(make, k):
        return lambda index: make(k, index).wait_recv()

    def begin(b, _):
        each(AROUND, None, start(h_first, b))
        each(AROUND, first, start(m_first, b))
        each(AROUND, first, start(x_first, b))
        each(AROUND, None, start(c_first, b))
        h_own_first(b).start()

        @pl.when(first)
        def _():
            m_own(b).start()
            x_own(b).start()

        return 0

    lax.fori_loop(0, batches, begin, 0)

    def begin_later(k, _):
        each(AROUND, first, start(x_first, k))
        pl.when(first)(lambda: x_own(k).start())
        return 0

    lax.fori_loop(batches, items, begin_later, 0)
    def unpack(window):
        for r in range(wr):
            value = window[r].astype(f32)
            turned = pltpu.roll(value, CH, 1)
            wide[r, pl.ds(SIDE, 16), :] = jnp.where(low, value, turned)
            wide[r, pl.ds(SIDE + 16, 16), :] = jnp.where(low, turned, value)
        for base, column in ((wr, SIDE - EDGE), (wr + 4, SIDE + tc)):
            for slab, (lo, hi) in enumerate(WINDOW_ROWS):
                value = window[base + slab].astype(f32)
                turned = pltpu.roll(value, CH, 1)
                upper = jnp.where(low, value, turned)
                lower = jnp.where(low, turned, value)
                for n in (0, 1):
                    wide[lo[n], pl.ds(column, EDGE), :] = upper[n * EDGE : (n + 1) * EDGE]
                    wide[hi[n], pl.ds(column, EDGE), :] = lower[n * EDGE : (n + 1) * EDGE]

    def spread():
        def tap(r, q):
            return wide[r, pl.ds(SIDE - EDGE - 2 + q, gc), :]

        for r in range(wr):
            taps = [tap(r, q) for q in range(KS)]
            p01[r] = jnp.where(low, taps[0], taps[1]).astype(bf16)
            p23[r] = jnp.where(low, taps[2], taps[3]).astype(bf16)
            p12[r] = jnp.where(low, taps[1], taps[2]).astype(bf16)
            p34[r] = jnp.where(low, taps[3], taps[4]).astype(bf16)
            p40[r] = jnp.where(low, taps[4], tap(min(r + 1, wr - 1), 0)).astype(bf16)

    def patches():
        parts = []
        for p in (0, 2):
            for buffer, at in ((p01, p), (p23, p), (p40, p), (p12, p + 1), (p34, p + 1)):
                parts.append(buffer[at : at + gr].reshape(gr * gc, 128))
        parts.append(p01[4 : 4 + gr].reshape(gr * gc, 128))
        parts.append(p23[4 : 4 + gr].reshape(gr * gc, 128))
        parts.append(p40[4 : 4 + gr].reshape(gr * gc, 128)[:, :CH])
        return jnp.concatenate(parts, axis=1)

    def arrived(k, copies):
        @pl.when(k == 0)
        def _():
            for copy in copies:
                copy.wait()

    bias = jnp.where(low, 0.0, 1.0)

    def cell(k, _):
        b = lax.rem(k, batches)
        early = k < batches
        late = k >= batches

        each_source(AROUND, early, landed(h_first, b))
        each_source(AROUND, late, landed(h_next, b))
        pl.when(early)(lambda: h_own_first(b).wait())
        pl.when(late)(lambda: h_own(b).wait())
        arrived(k, in_wh)
        unpack(hwin.at[k])
        spread()
        acc_h[...] = dot_rows(patches(), wh[...])

        @pl.when(early)
        def _():
            each_source(AROUND, None, landed(c_first, b))
            unpack(cwin.at[b])
            for r in range(gr):
                state[b, r] = wide[r + HALO - 2, pl.ds(SIDE - EDGE, gc), :]
            for r in range(tr):
                state[b, r + 2, pl.ds(EDGE, tc), :] = cel_ref[b, r]

        each_source(AROUND, first & early, landed(m_first, b))
        pl.when(first & early)(lambda: m_own(b).wait())
        each_source(EVERY, jnp.logical_not(first) | late, landed(m_next, k))
        arrived(k, in_wm)
        unpack(mwin.at[k])
        spread()
        acc_m[...] = dot_last(patches(), wm[...])
        for r in range(gr):
            memory[r] = wide[r + HALO - 2, pl.ds(SIDE - EDGE, gc), :]

        each_source(AROUND, first, landed(x_first, k))
        pl.when(first)(lambda: x_own(k).wait())
        each_source(EVERY, jnp.logical_not(first), landed(x_next, k))
        arrived(k, in_wxm + in_wxc)
        unpack(xwin.at[k])
        spread()
        acc_m[...] += dot_last(patches(), wxm[...])
        acc_h[...] += dot_last(patches(), wxc[...])

        for r in range(gr):
            span = slice(r * gc, (r + 1) * gc)
            gates = sigmoid(acc_m[span, :128] + bias)
            fresh_memory[r] = turn(gates) * memory[r] + gates * jnp.tanh(acc_m[span, 128:])
        pack_into(mbuf, k, lambda r: fresh_memory[r + 2, pl.ds(EDGE, tc), :], merge_low)
        each(EVERY, jnp.logical_not(last), start(m_next, k))
        each(EVERY, last & early, start(m_loop, k))

        grid_col = lax.broadcasted_iota(jnp.int32, (gc, 1), 0) + (col * tc - EDGE)
        col_ok = (grid_col >= 0) & (grid_col < cols * tc)
        for r in range(gr):
            span = slice(r * gc, (r + 1) * gc)
            gates = sigmoid(acc_h[span, :128] + bias)
            new = turn(gates) * state[b, r] + gates * jnp.tanh(acc_h[span, 128:])
            state[b, r] = new
            grid_row = row * tr + (r - 2)
            ok = col_ok & ((grid_row >= 0) & (grid_row < rows * tr))
            joined[r] = jnp.where(ok, jnp.where(low, new, turn(fresh_memory[r])), 0.0)

        arrived(k, in_wo)
        for q in range(KS):
            for r in range(gr):
                js[q, r] = joined[r, pl.ds(EDGE - 2 + q, tc), :].astype(bf16)
        parts = [
            js[q, 4 * g : 4 * g + tr + 3].reshape((tr + 3) * tc, 128)
            for g in range(2)
            for q in range(KS)
        ]
        out = dot_last(jnp.concatenate(parts, axis=1), wo[...])
        mixed = dot_last(js[2, 2 : 2 + tr].reshape(tr * tc, 128), wmix[...])
        hidden = []
        for r in range(tr):
            grid = slice((r + 2) * gc + EDGE, (r + 2) * gc + EDGE + tc)
            line = [slice((r + n) * tc, (r + n + 1) * tc) for n in range(4)]
            gate = out[line[1], :128] + out[line[3], 128:] + acc_h[grid, 128:]
            gate += turn(out[line[0], :128] + out[line[2], 128:])
            hidden.append(sigmoid(gate) * jnp.tanh(mixed[r * tc : (r + 1) * tc]))
        pack_into(hbuf, k, lambda r: hidden[r], merge_high)
        each(EVERY, jnp.logical_not(last), start(x_next, k))

        @pl.when(early)
        def _():
            each(AROUND, None, start(h_next, k))
            h_own(k).start()

        @pl.when(late)
        def _():
            for r in range(tr):
                outh_ref[b, r] = hidden[r]
            outs_ref[b] = joined[2 : 2 + tr, EDGE : EDGE + tc, :]

        return 0

    lax.fori_loop(0, items, cell, 0)

    def finish(k, _):
        each(AROUND, first, sent(x_first, k))
        each(EVERY, jnp.logical_not(last), sent(x_next, k))
        each(EVERY, jnp.logical_not(last), sent(m_next, k))
        return 0

    def finish_early(b, _):
        each(AROUND, first, sent(m_first, b))
        each(EVERY, last, sent(m_loop, b))
        each(AROUND, None, sent(h_first, b))
        each(AROUND, None, sent(h_next, b))
        each(AROUND, None, sent(c_first, b))
        return 0

    lax.fori_loop(0, items, finish, 0)
    lax.fori_loop(0, batches, finish_early, 0)


def per_device(
    sizes,
    frames,
    region_order,
    encoder,
    input_kernel,
    hidden_kernel,
    memory_kernel,
    output_kernel,
    mixing_weight,
    hidden_start,
    cell_start,
    memory_start,
):
    bf16, f32 = jnp.bfloat16, jnp.float32
    sections, rows, cols = sizes
    steps, _, patch, tr, tc = frames.shape
    batches, ch = memory_start.shape[:2]
    items = steps * batches
    gr, gc = tr + 4, tc + 2 * EDGE
    wr, wc = tr + 2 * HALO, tc + 2 * SIDE
    taps = KS * KS * ch

    def twice(value):
        return jnp.concatenate([value, value], -1)

    picked = jnp.take(frames, region_order[:batches], axis=1)
    enc = jnp.einsum(
        "tbcyx,oc->tbyxo", picked, twice(encoder.T).T, preferred_element_type=f32
    )
    enc = enc.astype(bf16).reshape(items, tr, tc, 2 * ch)
    hid = twice(hidden_start[0].transpose(0, 2, 3, 1).astype(bf16))
    cel = twice(cell_start[0].transpose(0, 2, 3, 1))
    mem = twice(memory_start.transpose(0, 2, 3, 1).astype(bf16))

    vmem = pl.BlockSpec(memory_space=pltpu.VMEM)
    anywhere = pl.BlockSpec(memory_space=pl.ANY)
    dma = pltpu.SemaphoreType.DMA
    window, packed = (wr + 8, 16, 128), (tr + 8, 16, 128)
    ends = jax.ShapeDtypeStruct((batches, tr, tc, 2 * ch), f32)
    outh, outs = pl.pallas_call(
        functools.partial(kernel_body, sections, rows, cols, steps, batches),
        out_shape=(ends, ends),
        in_specs=[anywhere] * 9,
        out_specs=(vmem, vmem),
        scratch_shapes=[
            pltpu.VMEM((items,) + window, bf16),
            pltpu.VMEM((items,) + window, bf16),
            pltpu.VMEM((items,) + window, bf16),
            pltpu.VMEM((batches,) + window, bf16),
            pltpu.VMEM((items,) + packed, bf16),
            pltpu.VMEM((batches,) + packed, bf16),
            pltpu.VMEM((batches,) + packed, bf16),
            pltpu.VMEM((batches,) + packed, bf16),
            pltpu.VMEM((items,) + packed, bf16),
            pltpu.VMEM((items,) + packed, bf16),
            pltpu.VMEM((wr, wc, 128), f32),
        ]
        + [pltpu.VMEM((wr, gc, 128), bf16)] * 5
        + [
            pltpu.VMEM((gr * gc, 256), f32),
            pltpu.VMEM((gr * gc, 256), f32),
            pltpu.VMEM((batches, gr, gc, 128), f32),
            pltpu.VMEM((gr, gc, 128), f32),
            pltpu.VMEM((gr, gc, 128), f32),
            pltpu.VMEM((gr, gc, 128), f32),
            pltpu.VMEM((KS, gr + 3, tc, 128), bf16),
            pltpu.VMEM(enc.shape, bf16),
            pltpu.VMEM(hid.shape, bf16),
            pltpu.VMEM(cel.shape, f32),
            pltpu.VMEM(mem.shape, bf16),
            pltpu.VMEM((4 * ch, taps), bf16),
            pltpu.VMEM((4 * ch, taps), bf16),
            pltpu.VMEM((taps, 4 * ch), bf16),
            pltpu.VMEM((4 * ch, taps), bf16),
            pltpu.VMEM((4 * ch, 2 * KS * 2 * ch), bf16),
            pltpu.VMEM((2 * ch, 2 * ch), bf16),
            dma((24,)),
            dma((items, 9)),
            dma((batches, 9)),
            dma((batches, 9)),
            dma((items, 9)),
            dma((items, 9)),
            dma((items, 9)),
            dma((items, 9)),
            dma((batches, 9)),
            dma((items, 9)),
            dma((batches, 9)),
            dma((batches, 9)),
            dma((4, items)),
        ],
        compiler_params=pltpu.CompilerParams(
            collective_id=0, has_side_effects=True, vmem_limit_bytes=67_043_328
        ),
        name="predrnn",
    )(
        enc,
        hid,
        cel,
        mem,
        input_kernel[0],
        hidden_kernel[0].T,
        memory_kernel[0],
        output_kernel[0],
        mixing_weight[0],
    )

    def back(value):
        return value.transpose(0, 3, 1, 2)[None]

    return back(outh[..., ch:]), back(outs[..., :ch]), back(outs[..., ch:])


def solution(mesh):
    sizes = tuple(mesh.shape[name] for name in ("section", "row", "col"))
    return jax.shard_map(
        functools.partial(per_device, sizes),
        mesh=mesh,
        in_specs=(
            P(None, None, None, "row", "col"),
            P(),
            P(),
            P("section", None, None),
            P("section", None, None),
            P("section", None, None),
            P("section", None, None),
            P("section", None, None),
            P("section", None, None, "row", "col"),
            P("section", None, None, "row", "col"),
            P(None, None, "row", "col"),
        ),
        out_specs=(
            P("section", None, None, "row", "col"),
            P("section", None, None, "row", "col"),
            P("section", None, None, "row", "col"),
        ),
        check_vma=False,
    )
```
